512 devices in a mesh: rhs: 64 (over x, z, core), row: 8 (over y).
Axes of the slice: x: 4, y: 8, z: 8, core: 2. Of those that a mesh axis runs over, the one named last changes fastest.
Arguments:
- rhs_block: float32 [4096, 16384], P('row', 'rhs'), may hold values from -6 to 6
- below: float32 [64, 4096, 512], P('rhs', 'row'), may hold values from -0.25 to 0.25
- inverse: float32 [64, 512, 512], P('rhs', 'row'), may hold values from -0.25 to 0.25
- owner_map: int32 [64], replicated, may hold values from 0 to 63, each once
- row_perm: int32 [4096], P('row'), may hold values from 0 to 4095, as said below
Outputs:
- solved_front: float32 [4096, 16384], P('row', 'rhs')
The draws below stay inside these ranges and needn't reach their ends.
Inputs may be any that keep to these rules, and one draw needn't show every extreme that they name: `owner_map`: entries 0 to 2 name the slots of the panels; all entries are distinct. `row_perm`: A permutation of the 4096 rows that maps each aligned block of 512 rows onto itself.
All inputs are finite; a program needn't handle non-finite values.
Results may differ from the reference program's by a relative error of at most 0.00013.
Values sent between devices are 32-bit elements; how exact they have to be, the bound alone decides.
No kernel may reach another device: no remote copies, remote signals or barrier semaphores. Data moves between devices by JAX's collectives and lax.ppermute only.
A program may use at most 64 MiB of HBM per device.

```python
import jax
import jax.numpy as jnp
from jax import lax

FRONT = 4096
PIVOTS = 512
PANELS = 3
NRHS = 16384
N_RHS = 64
N_ROW = 8


def draw_row_perm(key, part):
    block_rows = FRONT // N_ROW
    block_keys = jax.random.split(jax.random.fold_in(key, 7), N_ROW)
    blocks = jax.vmap(lambda single: jax.random.permutation(single, block_rows))(block_keys)
    offsets = jnp.arange(N_ROW, dtype=jnp.int32)[:, None] * block_rows
    return (blocks.astype(jnp.int32) + offsets).reshape(FRONT)


def steps_of(stream_key, shape, pieces, smallest, top_value):
    def one(dim, parts):
        heights = jax.random.uniform(jax.random.fold_in(jax.random.fold_in(stream_key, 6), dim), (parts,), jnp.float32, smallest / len(pieces), top_value / len(pieces))
        return jnp.repeat(jnp.exp(heights), shape[dim] // parts).reshape((-1,) + (1,) * (len(shape) - dim - 1))

    level = one(*pieces[0])
    for cut in pieces[1:]:
        level = level * one(*cut)
    return level


def normal_values(own_key, extent, spread, bound, cuts=(), held_as=jnp.bfloat16):
    factor_of = steps_of(own_key, extent, cuts, -0.22, 0.18) if cuts else 1.0
    drawn = jax.random.normal(own_key, extent, jnp.float32) * spread * factor_of
    return jnp.minimum(jnp.maximum(drawn, -bound), bound).astype(held_as)


def setup_inputs(seed: int = 0) -> dict:
    arg_keys = jax.random.split(jax.random.key(seed), 6)
    return {
        "rhs_block": normal_values(arg_keys[0], (FRONT, NRHS), 1.0, 6.0, ((0, 8), (1, 64)), jnp.float32),
        "below": normal_values(arg_keys[1], (N_RHS, FRONT, PIVOTS), PIVOTS ** -0.5, 0.25, ((0, 64), (1, 8)), jnp.float32),
        "inverse": normal_values(arg_keys[2], (N_RHS, PIVOTS, PIVOTS), PIVOTS ** -0.5, 0.25, ((0, 64), (1, 8)), jnp.float32),
        "owner_map": jax.random.permutation(arg_keys[3], N_RHS).astype(jnp.int32),
        "row_perm": draw_row_perm(jax.random.fold_in(arg_keys[5], 71), 0),
    }


def reference(rhs_block, below, inverse, owner_map, row_perm):
    rows_dev = FRONT // N_ROW
    slab_rows = PIVOTS // N_ROW
    columns = rhs_block.shape[1]
    working = jnp.take(rhs_block, row_perm, axis=0).reshape(N_ROW, rows_dev, columns)
    for panel_index in range(PANELS):
        holder = owner_map[panel_index]
        lower_rows = lax.dynamic_index_in_dim(below, holder, 0, keepdims=False).reshape(N_ROW, rows_dev, PIVOTS)
        inverse_block = lax.dynamic_index_in_dim(inverse, holder, 0, keepdims=False)
        first_row = panel_index * slab_rows
        last_row = first_row + slab_rows
        pivot_slab = working[:, first_row:last_row, :].reshape(PIVOTS, columns)
        solved = jnp.dot(inverse_block, pivot_slab, precision=lax.Precision.HIGHEST, preferred_element_type=jnp.float32)
        working = working.at[:, first_row:last_row, :].set(solved.reshape(N_ROW, slab_rows, columns))
        update = jnp.einsum("dip,pc->dic", lower_rows[:, last_row:, :], solved, precision=lax.Precision.HIGHEST)
        working = working.at[:, last_row:, :].add(-update)
    return working.reshape(FRONT, columns)
```

```python
import jax
import jax.numpy as jnp
from jax import lax
from jax.sharding import Mesh, PartitionSpec as P

PANELS = 3
ROW = "row"
PLANE = ("core", "x", "z")


def sent_to_all(x, axis):
    count = lax.axis_size(axis)
    return lax.all_to_all(jnp.broadcast_to(x[None], (count, *x.shape)), axis, 0, 0, tiled=True)


def dot(a, b):
    return jnp.dot(a, b, precision=lax.Precision.HIGHEST, preferred_element_type=jnp.float32)


def per_device(rhs_block, below, inverse, owner_map, row_perm):
    rows_dev, columns = rhs_block.shape
    slab = inverse.shape[1]
    pivots = inverse.shape[2]
    position = lax.axis_index(ROW)
    nx, nz, nc = lax.axis_size("x"), lax.axis_size("z"), lax.axis_size("core")
    plane = nx * nz * nc
    me = (lax.axis_index("x") * nz + lax.axis_index("z")) * nc + lax.axis_index("core")

    working = rhs_block.at[row_perm - position * rows_dev].get(mode="promise_in_bounds")
    pivot = sent_to_all(working[:slab], ROW).reshape(pivots, columns)

    whole_inverse = sent_to_all(inverse[0], ROW).reshape(pivots, pivots)
    operator = -dot(below[0], whole_inverse)
    panel_of_me = sum(jnp.where(owner_map[k] == me, k, 0) for k in range(PANELS))
    operator = lax.dynamic_update_slice(operator, inverse[0], (panel_of_me * slab, 0))

    piece = rows_dev // plane
    pieces = lax.all_to_all(operator.reshape(plane, piece, pivots), PLANE, 0, 0, tiled=True)
    kept = []
    for k in range(PANELS):
        o = owner_map[k]
        core, z, x = o % nc, (o // nc) % nz, o // (nc * nz)
        kept.append(lax.dynamic_index_in_dim(pieces, (core * nx + x) * nz + z, 0, keepdims=False))
    kept = jnp.stack(kept)
    kept = sent_to_all(kept, "z")
    kept = sent_to_all(kept, "x")
    mine = kept
    other = lax.ppermute(kept, "core", [(0, 1), (1, 0)])
    first = lax.axis_index("core") == 0
    halves = [jnp.where(first, mine, other), jnp.where(first, other, mine)]

    for k in range(PANELS):
        start, end = k * slab, (k + 1) * slab
        panel = jnp.concatenate([h[:, :, k].reshape(rows_dev // 2, pivots) for h in halves], axis=0)
        if k:
            pivot = sent_to_all(working[start:end], ROW).reshape(pivots, columns)
        moved = dot(panel[start:], pivot)
        working = jnp.concatenate(
            [working[:start], moved[:slab], working[end:] + moved[slab:]], axis=0
        )
    return working


def solution(mesh):
    mesh = Mesh(mesh.devices.reshape(4, 8, 2, 8), ("x", "z", "core", "row"))
    rhs = ("x", "z", "core")
    return jax.shard_map(
        per_device,
        mesh=mesh,
        in_specs=(P("row", rhs), P(rhs, "row", None), P(rhs, "row", None), P(), P("row")),
        out_specs=P("row", rhs),
        check_vma=False,
    )
```

```python
import jax
import jax.numpy as jnp
from jax import lax
from jax.sharding import Mesh, PartitionSpec as P

PANELS = 3
ROW = "row"
CHIP = ("x", "z")
PLANE = ("core", "x", "z")
SWAP = [(0, 1), (1, 0)]


def sent_to_all(x, axis):
    count = lax.axis_size(axis)
    return lax.all_to_all(jnp.broadcast_to(x[None], (count, *x.shape)), axis, 0, 0, tiled=True)


def dot(a, b):
    return jnp.dot(a, b, precision=lax.Precision.HIGHEST, preferred_element_type=jnp.float32)


def spread(operator, axes, sources):
    rows, pivots = operator.shape
    count = lax.axis_size(axes)
    operator, sources = lax.optimization_barrier((operator, sources))
    pieces = lax.all_to_all(operator.reshape(count, rows // count, pivots), axes, 0, 0, tiled=True)
    return jnp.stack([lax.dynamic_index_in_dim(pieces, s, 0, keepdims=False) for s in sources])


def shared_slots(below, inverse, core, own_core, panel, chips, sources):
    slab, pivots = inverse.shape
    rows = below.shape[0] // 2
    kept_rows = lax.dynamic_slice_in_dim(below, core * rows, rows, 0)
    sent_rows = lax.dynamic_slice_in_dim(below, (1 - core) * rows, rows, 0)
    got = lax.ppermute(jnp.concatenate([sent_rows, inverse]), "core", SWAP)
    mine = core == own_core
    lower = jnp.where(mine, kept_rows, got[:rows])
    slab_rows = jnp.where(mine, inverse, got[rows:])
    part = lax.dynamic_slice_in_dim(slab_rows, core * (slab // 2), slab // 2, 0)
    part = sent_to_all(part, ROW)
    other = lax.ppermute(part, "core", SWAP)
    first = core == 0
    whole = jnp.stack([jnp.where(first, part, other), jnp.where(first, other, part)], axis=1)
    operator = -dot(lower, whole.reshape(pivots, pivots))
    operator = jnp.where(
        first, lax.dynamic_update_slice(operator, slab_rows, (panel * slab, 0)), operator
    )
    return spread(operator, CHIP, chips)


def own_slots(below, inverse, core, own_core, panel, chips, sources):
    slab, pivots = inverse.shape
    whole = sent_to_all(inverse, ROW).reshape(pivots, pivots)
    operator = -dot(below, whole)
    operator = lax.dynamic_update_slice(operator, inverse, (panel * slab, 0))
    return spread(operator, PLANE, sources)


def per_device(rhs_block, below, inverse, owner_map, row_perm):
    rows_dev, columns = rhs_block.shape
    slab = inverse.shape[1]
    pivots = inverse.shape[2]
    position = lax.axis_index(ROW)
    core = lax.axis_index("core")
    chip = lax.axis_index(CHIP)
    count = lax.axis_size(CHIP)

    working = rhs_block.at[row_perm - position * rows_dev].get(mode="promise_in_bounds")
    pivot = sent_to_all(working[:slab], ROW).reshape(pivots, columns)

    owners = [owner_map[k] for k in range(PANELS)]
    chips = [o // 2 for o in owners]
    cores = [o % 2 for o in owners]
    sources = [(c * count + h).astype(jnp.uint32) for c, h in zip(cores, chips)]
    chip_sources = [h.astype(jnp.uint32) for h in chips]
    twice = (chips[0] == chips[1]) | (chips[0] == chips[2]) | (chips[1] == chips[2])
    own_core = sum(jnp.where(h == chip, c, 0) for c, h in zip(cores, chips))
    panel_chip = sum(jnp.where(h == chip, k, 0) for k, h in enumerate(chips))
    panel_core = sum(
        jnp.where((h == chip) & (c == core), k, 0) for k, (c, h) in enumerate(zip(cores, chips))
    )
    panel = jnp.where(twice, panel_core, panel_chip)
    kept = lax.cond(
        twice,
        own_slots,
        shared_slots,
        below[0],
        inverse[0],
        core,
        own_core,
        panel,
        chip_sources,
        sources,
    )

    kept = sent_to_all(kept, "z")
    kept = sent_to_all(kept, "x")
    other = lax.ppermute(kept, "core", SWAP)
    first = core == 0
    halves = [jnp.where(first, kept, other), jnp.where(first, other, kept)]

    for k in range(PANELS):
        start, end = k * slab, (k + 1) * slab
        panel = jnp.concatenate([h[:, :, k].reshape(rows_dev // 2, pivots) for h in halves], axis=0)
        if k:
            pivot = sent_to_all(working[start:end], ROW).reshape(pivots, columns)
        moved = dot(panel[start:], pivot)
        working = jnp.concatenate(
            [working[:start], moved[:slab], working[end:] + moved[slab:]], axis=0
        )
    return working


def solution(mesh):
    mesh = Mesh(mesh.devices.reshape(4, 8, 2, 8), ("x", "z", "core", "row"))
    rhs = ("x", "z", "core")
    return jax.shard_map(
        per_device,
        mesh=mesh,
        in_specs=(P("row", rhs), P(rhs, "row", None), P(rhs, "row", None), P(), P("row")),
        out_specs=P("row", rhs),
        check_vma=False,
    )
```

```python
import jax
import jax.numpy as jnp
from jax import lax
from jax.sharding import Mesh, PartitionSpec as P


PANELS = 3
ROW = "row"
CHIP = ("z", "x")
SWAP = [(0, 1), (1, 0)]


def sent_to_all(x, axis):
    count = lax.axis_size(axis)
    return lax.all_to_all(jnp.broadcast_to(x[None], (count, *x.shape)), axis, 0, 0, tiled=True)


def dot(a, b):
    return jnp.dot(a, b, precision=lax.Precision.HIGHEST, preferred_element_type=jnp.float32)


def both_cores(x, on_first):
    other = lax.ppermute(x, "core", SWAP)
    return jnp.where(on_first, x, other), jnp.where(on_first, other, x)


def spread(operator, sources, pivot):
    groups, across, piece, pivots = operator.shape
    operator, sources, pivot = lax.optimization_barrier((operator, sources, pivot))
    pieces = lax.all_to_all(
        operator.reshape(groups * across, piece, pivots), CHIP, 0, 0, tiled=True
    )
    kept = [lax.dynamic_index_in_dim(pieces, s, 0, keepdims=False) for s in sources]
    return jnp.stack(kept), pivot


def gathered(rows, pivot_rows):
    n, columns = rows.shape[0], pivot_rows.shape[1]
    both = jnp.concatenate([rows[:, :columns], rows[:, columns:], pivot_rows])
    both = sent_to_all(both, ROW)
    rows = jnp.concatenate([both[:, :n], both[:, n : 2 * n]], axis=2)
    return rows, both[:, 2 * n :].reshape(-1, columns)


def with_inverse(operator, rows, panel):
    group = lax.broadcasted_iota(jnp.int32, operator.shape, 0)
    return jnp.where(group == panel, rows[None], operator)


def shared_slots(below, inverse, pivot_rows, core, own_core, panel, panel_core, chips, cores):
    groups, _, half, pivots = below.shape
    inverse = inverse.reshape(1, 2, half, pivots)
    mixed = jnp.concatenate([below, inverse])
    on_first = core == 0
    kept = jnp.where(on_first, mixed[:, 0], mixed[:, 1])
    sent = jnp.where(on_first, mixed[:, 1], mixed[:, 0])
    got = lax.ppermute(sent, "core", SWAP)
    mixed = jnp.where(core == own_core, kept, got)
    part = mixed[groups]
    parts, pivot = gathered(part, pivot_rows)
    low, high = both_cores(parts, on_first)
    whole = jnp.stack([low, high], axis=1).reshape(pivots, pivots)
    operator = -dot(mixed[:groups].reshape(groups * half, pivots), whole)
    operator = with_inverse(operator.reshape(groups, half, pivots), part, panel)
    return spread(operator.reshape(groups, half // 8, 8, pivots), chips, pivot)


def own_slots(below, inverse, pivot_rows, core, own_core, panel, panel_core, chips, cores):
    groups, _, half, pivots = below.shape
    whole, pivot = gathered(inverse, pivot_rows)
    whole = whole.reshape(pivots, pivots)
    operator = -dot(below.reshape(groups * 2 * half, pivots), whole)
    operator = with_inverse(operator.reshape(groups, 2 * half, pivots), inverse, panel_core)
    operator = operator.reshape(groups, 2, half, pivots)
    on_first = core == 0
    mine = jnp.where(on_first, operator[:, 0], operator[:, 1])
    other = jnp.where(on_first, operator[:, 1], operator[:, 0])
    other = lax.ppermute(other, "core", SWAP)
    shape = (groups, half // 8, 8, pivots)
    mine, pivot = spread(mine.reshape(shape), chips, pivot)
    other, pivot = spread(other.reshape(shape), chips, pivot)
    kept = jnp.stack([jnp.where(c == core, mine[k], other[k]) for k, c in enumerate(cores)])
    return kept, pivot


def per_device(rhs_block, below, inverse, owner_map, row_perm):
    rows_dev, columns = rhs_block.shape
    slab, pivots = inverse.shape[1:]
    groups = rows_dev // slab
    position = lax.axis_index(ROW)
    core = lax.axis_index("core")
    nz, nx = lax.axis_size("z"), lax.axis_size("x")
    chip = (lax.axis_index("x") * nz + lax.axis_index("z")).astype(jnp.uint32)

    owners = [owner_map[k].astype(jnp.uint32) for k in range(PANELS)]
    chips = [o >> 1 for o in owners]
    cores = [(o & 1).astype(jnp.int32) for o in owners]
    twice = (chips[0] == chips[1]) | (chips[0] == chips[2]) | (chips[1] == chips[2])
    held = [h == chip for h in chips]
    own_core = jnp.where(held[0], cores[0], jnp.where(held[1], cores[1], cores[2]))
    panel = jnp.where(held[0], 0, jnp.where(held[1], 1, 2))
    panel_core = jnp.where(
        held[0] & (cores[0] == core), 0, jnp.where(held[1] & (cores[1] == core), 1, 2)
    )
    sources = [(h % nz) * nx + h // nz for h in chips]

    working = rhs_block.at[row_perm - position * rows_dev].get(mode="promise_in_bounds")
    kept, pivot = lax.cond(
        twice,
        own_slots,
        shared_slots,
        below[0].reshape(groups, 2, slab // 2, pivots),
        inverse[0],
        working[:slab],
        core,
        own_core,
        panel,
        panel_core,
        sources,
        cores,
    )

    pivot = [pivot]
    kept, on_first = lax.optimization_barrier((kept, core == 0))

    kept = sent_to_all(kept, "z")
    pairs = [(g, k) for g in range(PANELS) for k in range(g)] + [(k, k) for k in range(PANELS)]
    first = sent_to_all(jnp.stack([kept[g, k] for g, k in pairs]), "x")
    first = jnp.concatenate(both_cores(first, on_first))
    first = {at: first[:, n].reshape(slab, pivots) for n, at in enumerate(pairs)}
    rest = lax.all_gather(kept[PANELS:], "x")
    rest = jnp.concatenate(both_cores(rest, on_first))

    for g in range(1, PANELS):
        rows = working[g * slab : (g + 1) * slab]
        for k in range(g):
            rows = rows + dot(first[g, k], pivot[k])
        pivot.append(sent_to_all(rows, ROW).reshape(pivots, columns))

    tail = working[PANELS * slab :]
    pieces, left = rest.shape[:2]
    moved = sum(dot(rest[:, :, k].reshape(-1, pivots), pivot[k]) for k in range(PANELS))
    moved = moved.reshape(pieces, left, -1, columns).swapaxes(0, 1).reshape(tail.shape)
    solved = [dot(first[k, k], pivot[k]) for k in range(PANELS)]
    return jnp.concatenate([*solved, tail + moved])


def solution(mesh):
    mesh4 = Mesh(mesh.devices.reshape(4, 8, 2, 8), ("x", "z", "core", "row"))
    rhs = ("x", "z", "core")

    def step(*args):
        return per_device(*args)

    step = jax.shard_map(
        step,
        mesh=mesh4,
        in_specs=(P("row", rhs), P(rhs, "row", None), P(rhs, "row", None), P(), P("row")),
        out_specs=P("row", rhs),
        check_vma=False,
    )
    return step
```

```python
import jax
import jax.numpy as jnp
from jax import lax
from jax.sharding import Mesh, PartitionSpec as P


PANELS = 3
ROW = "row"
CHIP = ("z", "x")
SWAP = [(0, 1), (1, 0)]


def sent_to_all(x, axis):
    count = lax.axis_size(axis)
    return lax.all_to_all(jnp.broadcast_to(x[None], (count, *x.shape)), axis, 0, 0, tiled=True)


def dot(a, b):
    return jnp.dot(a, b, precision=lax.Precision.HIGHEST, preferred_element_type=jnp.float32)


def both_cores(x, on_first):
    other = lax.ppermute(x, "core", SWAP)
    return jnp.where(on_first, x, other), jnp.where(on_first, other, x)


def spread(operator, sources, pivot):
    groups, across, piece, pivots = operator.shape
    operator, sources, pivot = lax.optimization_barrier((operator, sources, pivot))
    pieces = lax.all_to_all(
        operator.reshape(groups * across, piece, pivots), CHIP, 0, 0, tiled=True
    )
    kept = [lax.dynamic_index_in_dim(pieces, s, 0, keepdims=False) for s in sources]
    return jnp.stack(kept), pivot


def permuted(rhs_block, row_perm):
    position = lax.axis_index(ROW)
    rows = row_perm - position * rhs_block.shape[0]
    return rhs_block.at[rows].get(mode="promise_in_bounds")


def with_inverse(operator, rows, panel):
    group = lax.broadcasted_iota(jnp.int32, operator.shape, 0)
    return jnp.where(group == panel, rows[None], operator)


def shared_slots(below, inverse, rhs_block, row_perm, core, own_core, panel, panel_core, chips, cores):
    groups, _, half, pivots = below.shape
    inverse = inverse.reshape(2, half, pivots)
    on_first, mine = core == 0, core == own_core
    sent = jnp.where(on_first, inverse[1], inverse[0])
    kept = jnp.where(on_first, inverse[0], inverse[1])
    part = jnp.where(mine, kept, lax.ppermute(sent, "core", SWAP))
    sent = jnp.where(on_first, below[:, 1], below[:, 0])
    kept = jnp.where(on_first, below[:, 0], below[:, 1])
    lower = jnp.where(mine, kept, lax.ppermute(sent, "core", SWAP))
    working = permuted(rhs_block, row_perm)
    pivot = sent_to_all(working[: 2 * half], ROW).reshape(pivots, -1)
    parts = lax.all_gather(part, ROW)
    low, high = both_cores(parts, on_first)
    whole = jnp.stack([low, high], axis=1).reshape(pivots, pivots)
    operator = -dot(lower.reshape(groups * half, pivots), whole)
    operator = with_inverse(operator.reshape(groups, half, pivots), part, panel)
    kept, pivot = spread(operator.reshape(groups, half // 8, 8, pivots), chips, pivot)
    return kept, pivot, working


def own_slots(below, inverse, rhs_block, row_perm, core, own_core, panel, panel_core, chips, cores):
    groups, _, half, pivots = below.shape
    working = permuted(rhs_block, row_perm)
    pivot = sent_to_all(working[: 2 * half], ROW).reshape(pivots, -1)
    whole = sent_to_all(inverse, ROW).reshape(pivots, pivots)
    operator = -dot(below.reshape(groups * 2 * half, pivots), whole)
    operator = with_inverse(operator.reshape(groups, 2 * half, pivots), inverse, panel_core)
    operator = operator.reshape(groups, 2, half, pivots)
    on_first = core == 0
    mine = jnp.where(on_first, operator[:, 0], operator[:, 1])
    other = jnp.where(on_first, operator[:, 1], operator[:, 0])
    other = lax.ppermute(other, "core", SWAP)
    shape = (groups, half // 8, 8, pivots)
    mine, pivot = spread(mine.reshape(shape), chips, pivot)
    other, pivot = spread(other.reshape(shape), chips, pivot)
    kept = jnp.stack([jnp.where(c == core, mine[k], other[k]) for k, c in enumerate(cores)])
    return kept, pivot, working


def per_device(rhs_block, below, inverse, owner_map, row_perm):
    rows_dev, columns = rhs_block.shape
    slab, pivots = inverse.shape[1:]
    groups = rows_dev // slab
    core = lax.axis_index("core")
    nz, nx = lax.axis_size("z"), lax.axis_size("x")
    chip = (lax.axis_index("x") * nz + lax.axis_index("z")).astype(jnp.uint32)

    owners = [owner_map[k].astype(jnp.uint32) for k in range(PANELS)]
    chips = [o >> 1 for o in owners]
    cores = [(o & 1).astype(jnp.int32) for o in owners]
    twice = (chips[0] == chips[1]) | (chips[0] == chips[2]) | (chips[1] == chips[2])
    held = [h == chip for h in chips]
    own_core = jnp.where(held[0], cores[0], jnp.where(held[1], cores[1], cores[2]))
    panel = jnp.where(held[0], 0, jnp.where(held[1], 1, 2))
    panel_core = jnp.where(
        held[0] & (cores[0] == core), 0, jnp.where(held[1] & (cores[1] == core), 1, 2)
    )
    sources = [(h % nz) * nx + h // nz for h in chips]

    kept, pivot, working = lax.cond(
        twice,
        own_slots,
        shared_slots,
        below[0].reshape(groups, 2, slab // 2, pivots),
        inverse[0],
        rhs_block,
        row_perm,
        core,
        own_core,
        panel,
        panel_core,
        sources,
        cores,
    )

    pivot = [pivot]
    kept, on_first = lax.optimization_barrier((kept, core == 0))

    kept = sent_to_all(kept, "z")
    pairs = [(g, k) for g in range(PANELS) for k in range(g)] + [(k, k) for k in range(PANELS)]
    first = sent_to_all(jnp.stack([kept[g, k] for g, k in pairs]), "x")
    first = jnp.concatenate(both_cores(first, on_first))
    first = {at: first[:, n].reshape(slab, pivots) for n, at in enumerate(pairs)}
    rest = lax.all_gather(kept[PANELS:], "x")
    rest = rest, lax.ppermute(rest, "core", SWAP)

    for g in range(1, PANELS):
        rows = working[g * slab : (g + 1) * slab]
        for k in range(g):
            rows = rows + dot(first[g, k], pivot[k])
        pivot.append(sent_to_all(rows, ROW).reshape(pivots, columns))

    tail = working[PANELS * slab :]
    here, there = (
        sum(dot(r[:, :, k].reshape(-1, pivots), pivot[k]) for k in range(PANELS)) for r in rest
    )
    moved = jnp.stack([jnp.where(on_first, here, there), jnp.where(on_first, there, here)])
    pieces, left = rest[0].shape[:2]
    moved = moved.reshape(2 * pieces, left, -1, columns).swapaxes(0, 1).reshape(tail.shape)
    solved = [dot(first[k, k], pivot[k]) for k in range(PANELS)]
    return jnp.concatenate([*solved, tail + moved])


def solution(mesh):
    mesh4 = Mesh(mesh.devices.reshape(4, 8, 2, 8), ("x", "z", "core", "row"))
    rhs = ("x", "z", "core")

    def step(*args):
        return per_device(*args)

    step = jax.shard_map(
        step,
        mesh=mesh4,
        in_specs=(P("row", rhs), P(rhs, "row", None), P(rhs, "row", None), P(), P("row")),
        out_specs=P("row", rhs),
        check_vma=False,
    )
    return step
```

```python
import jax
import jax.numpy as jnp
from jax import lax
from jax.sharding import Mesh, PartitionSpec as P


PANELS = 3
ROW = "row"
CHIP = ("z", "x")
SWAP = [(0, 1), (1, 0)]


def sent_to_all(x, axis):
    count = lax.axis_size(axis)
    return lax.all_to_all(jnp.broadcast_to(x[None], (count, *x.shape)), axis, 0, 0, tiled=True)


def dot(a, b):
    return jnp.dot(a, b, precision=lax.Precision.HIGHEST, preferred_element_type=jnp.float32)


def both_cores(x, on_first):
    other = lax.ppermute(x, "core", SWAP)
    return jnp.where(on_first, x, other), jnp.where(on_first, other, x)


def spread(operator, sources):
    groups, across, piece, pivots = operator.shape
    operator, sources = lax.optimization_barrier((operator, sources))
    pieces = lax.all_to_all(
        operator.reshape(groups * across, piece, pivots), CHIP, 0, 0, tiled=True
    )
    return jnp.stack([lax.dynamic_index_in_dim(pieces, s, 0, keepdims=False) for s in sources])


def with_inverse(operator, rows, panel):
    group = lax.broadcasted_iota(jnp.int32, operator.shape, 0)
    return jnp.where(group == panel, rows[None], operator)


def shared_slots(below, inverse, core, own_core, panel, panel_core, chips, cores):
    groups, _, half, pivots = below.shape
    inverse = inverse.reshape(1, 2, half, pivots)
    mixed = jnp.concatenate([below, inverse])
    on_first = core == 0
    kept = jnp.where(on_first, mixed[:, 0], mixed[:, 1])
    sent = jnp.where(on_first, mixed[:, 1], mixed[:, 0])
    got = lax.ppermute(sent, "core", SWAP)
    mixed = jnp.where(core == own_core, kept, got)
    part = mixed[groups]
    low, high = both_cores(sent_to_all(part, ROW), on_first)
    whole = jnp.stack([low, high], axis=1).reshape(pivots, pivots)
    operator = -dot(mixed[:groups].reshape(groups * half, pivots), whole)
    operator = with_inverse(operator.reshape(groups, half, pivots), part, panel)
    return spread(operator.reshape(groups, half // 8, 8, pivots), chips)


def own_slots(below, inverse, core, own_core, panel, panel_core, chips, cores):
    groups, _, half, pivots = below.shape
    whole = sent_to_all(inverse, ROW).reshape(pivots, pivots)
    operator = -dot(below.reshape(groups * 2 * half, pivots), whole)
    operator = with_inverse(operator.reshape(groups, 2 * half, pivots), inverse, panel_core)
    operator = operator.reshape(groups, 2, half, pivots)
    on_first = core == 0
    mine = jnp.where(on_first, operator[:, 0], operator[:, 1])
    other = jnp.where(on_first, operator[:, 1], operator[:, 0])
    other = lax.ppermute(other, "core", SWAP)
    shape = (groups, half // 8, 8, pivots)
    mine = spread(mine.reshape(shape), chips)
    other = spread(other.reshape(shape), chips)
    return jnp.stack([jnp.where(c == core, mine[k], other[k]) for k, c in enumerate(cores)])


def per_device(rhs_block, below, inverse, owner_map, row_perm):
    rows_dev, columns = rhs_block.shape
    slab, pivots = inverse.shape[1:]
    groups = rows_dev // slab
    position = lax.axis_index(ROW)
    core = lax.axis_index("core")
    nz, nx = lax.axis_size("z"), lax.axis_size("x")
    chip = (lax.axis_index("x") * nz + lax.axis_index("z")).astype(jnp.uint32)

    owners = [owner_map[k].astype(jnp.uint32) for k in range(PANELS)]
    chips = [o >> 1 for o in owners]
    cores = [(o & 1).astype(jnp.int32) for o in owners]
    twice = (chips[0] == chips[1]) | (chips[0] == chips[2]) | (chips[1] == chips[2])
    held = [h == chip for h in chips]
    own_core = jnp.where(held[0], cores[0], jnp.where(held[1], cores[1], cores[2]))
    panel = jnp.where(held[0], 0, jnp.where(held[1], 1, 2))
    panel_core = jnp.where(
        held[0] & (cores[0] == core), 0, jnp.where(held[1] & (cores[1] == core), 1, 2)
    )
    sources = [(h % nz) * nx + h // nz for h in chips]

    kept = lax.cond(
        twice,
        own_slots,
        shared_slots,
        below[0].reshape(groups, 2, slab // 2, pivots),
        inverse[0],
        core,
        own_core,
        panel,
        panel_core,
        sources,
        cores,
    )

    kept, on_first = lax.optimization_barrier((kept, core == 0))

    def permuted(start, end):
        rows = row_perm[start:end] - position * rows_dev
        return rhs_block.at[rows].get(mode="promise_in_bounds")

    def to_all_rows(rows):
        return sent_to_all(rows, ROW).reshape(pivots, columns)

    kept = sent_to_all(kept, "z")
    pivot = [to_all_rows(permuted(0, slab))]
    working = permuted(slab, rows_dev)
    pairs = [(g, k) for g in range(PANELS) for k in range(g + 1)]
    first = lax.all_gather(jnp.stack([kept[g, k] for g, k in pairs]), "x")
    first = jnp.concatenate(both_cores(first, on_first))
    first = {at: first[:, n].reshape(slab, pivots) for n, at in enumerate(pairs)}
    parts = []
    for start, end in [(PANELS, groups - 2), (groups - 2, groups)]:
        rest = lax.all_gather(kept[start:end], "x")
        parts.append(jnp.concatenate(both_cores(rest, on_first)))

    for g in range(1, PANELS):
        rows = working[(g - 1) * slab : g * slab]
        for k in range(g):
            rows = rows + dot(first[g, k], pivot[k])
        pivot.append(to_all_rows(rows))

    tail = []
    for rest in parts:
        pieces, left = rest.shape[:2]
        moved = sum(dot(rest[:, :, k].reshape(-1, pivots), pivot[k]) for k in range(PANELS))
        moved = moved.reshape(pieces, left, -1, columns).swapaxes(0, 1)
        tail.append(moved.reshape(left * slab, columns))
    tail = working[(PANELS - 1) * slab :] + jnp.concatenate(tail)
    solved = [dot(first[k, k], pivot[k]) for k in range(PANELS)]
    return jnp.concatenate([*solved, tail])


def solution(mesh):
    mesh4 = Mesh(mesh.devices.reshape(4, 8, 2, 8), ("x", "z", "core", "row"))
    rhs = ("x", "z", "core")

    def step(*args):
        return per_device(*args)

    step = jax.shard_map(
        step,
        mesh=mesh4,
        in_specs=(P("row", rhs), P(rhs, "row", None), P(rhs, "row", None), P(), P("row")),
        out_specs=P("row", rhs),
        check_vma=False,
    )
    return step
```

```python
import jax
import jax.numpy as jnp
from jax import lax
from jax.sharding import Mesh, PartitionSpec as P


PANELS = 3
ROW = "row"
CHIP = ("z", "x")
SWAP = [(0, 1), (1, 0)]


def sent_to_all(x, axis):
    count = lax.axis_size(axis)
    return lax.all_to_all(jnp.broadcast_to(x[None], (count, *x.shape)), axis, 0, 0, tiled=True)


def swapped(x):
    return lax.ppermute(x, "core", SWAP)


def dot(a, b):
    return jnp.dot(a, b, precision=lax.Precision.HIGHEST, preferred_element_type=jnp.float32)


def halves(x, on_first, axis):
    low, high = jnp.split(x, 2, axis)
    return jnp.where(on_first, low, high), jnp.where(on_first, high, low)


def spread(operator, sources):
    rows, columns = operator.shape
    count = lax.axis_size(CHIP)
    operator, sources = lax.optimization_barrier((operator, sources))
    pieces = lax.all_to_all(
        operator.reshape(count, rows // count, columns), CHIP, 0, 0, tiled=True
    )
    return jnp.stack([lax.dynamic_index_in_dim(pieces, s, 0, keepdims=False) for s in sources])


def operator_of(below, inverse, own_rows, panel):
    slab = own_rows.shape[0]
    product = -dot(below, inverse)
    group = lax.broadcasted_iota(jnp.int32, product.shape, 0) // slab
    return jnp.where(group == panel, jnp.tile(own_rows, (below.shape[0] // slab, 1)), product)


def shared_slots(lower, whole, part, below, inverse, on_first, panel, panel_core, sources, cores):
    return spread(operator_of(lower, whole, part, panel), sources)


def own_slots(lower, whole, part, below, inverse, on_first, panel, panel_core, sources, cores):
    whole = sent_to_all(inverse, ROW).reshape(-1, inverse.shape[1])
    mine, other = halves(operator_of(below, whole, inverse, panel_core), on_first, 1)
    mine, other = spread(mine, sources), spread(swapped(other), sources)
    here = [(c == 0) == on_first for c in cores]
    return jnp.stack([jnp.where(h, mine[k], other[k]) for k, h in enumerate(here)])


def per_device(rhs_block, below, inverse, owner_map, row_perm):
    rows_dev, columns = rhs_block.shape
    below, inverse = below[0], inverse[0]
    slab, pivots = inverse.shape
    position = lax.axis_index(ROW)
    core = lax.axis_index("core")
    on_first = core == 0
    nz, nx = lax.axis_size("z"), lax.axis_size("x")
    chip = (lax.axis_index("x") * nz + lax.axis_index("z")).astype(jnp.uint32)

    owners = [owner_map[k].astype(jnp.uint32) for k in range(PANELS)]
    chips = [o >> 1 for o in owners]
    cores = [(o & 1).astype(jnp.int32) for o in owners]
    twice = (chips[0] == chips[1]) | (chips[0] == chips[2]) | (chips[1] == chips[2])
    held = [h == chip for h in chips]
    own_core = jnp.where(held[0], cores[0], jnp.where(held[1], cores[1], cores[2]))
    panel = jnp.where(held[0], 0, jnp.where(held[1], 1, 2))
    panel_core = jnp.where(
        held[0] & (cores[0] == core), 0, jnp.where(held[1] & (cores[1] == core), 1, 2)
    )
    sources = [(h % nz) * nx + h // nz for h in chips]

    kept, sent = halves(inverse, on_first, 1)
    part = jnp.where(own_core == core, kept, swapped(sent))
    lower = jnp.where(own_core == core, below, swapped(below))
    whole = sent_to_all(part, ROW).reshape(pivots, -1)
    kept = lax.cond(
        twice,
        own_slots,
        shared_slots,
        lower,
        whole,
        part,
        below,
        inverse,
        on_first,
        panel,
        panel_core,
        sources,
        cores,
    )

    def permuted(start, end):
        rows = row_perm[start:end] - position * rows_dev
        return rhs_block.at[rows].get(mode="promise_in_bounds")

    def to_all_rows(rows):
        return halves(sent_to_all(rows, ROW).reshape(pivots, columns), on_first, 0)

    def product(a, b):
        return dot(a[0], b[0]) + dot(a[1], b[1])

    kept = sent_to_all(kept, "z")
    pivot = [to_all_rows(permuted(0, slab))]
    working = permuted(slab, rows_dev)
    pairs = [(g, k) for g in range(PANELS) for k in range(g + 1)]
    first = lax.all_gather(jnp.stack([kept[g, k] for g, k in pairs]), "x")
    first = first, swapped(first)
    first = {
        at: [f[:, n].reshape(slab, pivots // 2) for f in first] for n, at in enumerate(pairs)
    }
    rest = lax.all_gather(kept[PANELS:], "x")
    rest = rest, swapped(rest)

    for g in range(1, PANELS):
        rows = working[(g - 1) * slab : g * slab]
        for k in range(g):
            rows = rows + product(first[g, k], pivot[k])
        pivot.append(to_all_rows(rows))

    moved = sum(
        product([r[:, :, k].reshape(-1, pivots // 2) for r in rest], pivot[k])
        for k in range(PANELS)
    )
    pieces, left = rest[0].shape[:2]
    moved = moved.reshape(pieces, left, -1, columns).swapaxes(0, 1).reshape(-1, columns)
    solved = [product(first[k, k], pivot[k]) for k in range(PANELS)]
    return jnp.concatenate([*solved, working[(PANELS - 1) * slab :] + moved])


def solution(mesh):
    mesh4 = Mesh(mesh.devices.reshape(4, 8, 2, 8), ("x", "z", "core", "row"))
    rhs = ("x", "z", "core")

    def step(*args):
        return per_device(*args)

    step = jax.shard_map(
        step,
        mesh=mesh4,
        in_specs=(P("row", rhs), P(rhs, "row", None), P(rhs, "row", None), P(), P("row")),
        out_specs=P("row", rhs),
        check_vma=False,
    )
    return step
```

```python
import jax
import jax.numpy as jnp
from jax import lax
from jax.sharding import Mesh, PartitionSpec as P


PANELS = 3
ROW = "row"
CHIP = ("z", "x")
SWAP = [(0, 1), (1, 0)]


def sent_to_all(x, axis):
    count = lax.axis_size(axis)
    return lax.all_to_all(jnp.broadcast_to(x[None], (count, *x.shape)), axis, 0, 0, tiled=True)


def swapped(x):
    return lax.ppermute(x, "core", SWAP)


def dot(a, b):
    return jnp.dot(a, b, precision=lax.Precision.HIGHEST, preferred_element_type=jnp.float32)


def halves(x, on_first, axis):
    low, high = jnp.split(x, 2, axis)
    return jnp.where(on_first, low, high), jnp.where(on_first, high, low)


def spread(operator, sources):
    rows, columns = operator.shape
    count = lax.axis_size(CHIP)
    operator, sources = lax.optimization_barrier((operator, sources))
    pieces = lax.all_to_all(
        operator.reshape(count, rows // count, columns), CHIP, 0, 0, tiled=True
    )
    return jnp.stack([lax.dynamic_index_in_dim(pieces, s, 0, keepdims=False) for s in sources])


def operator_of(below, inverse, own_rows, panel):
    slab = own_rows.shape[0]
    product = -dot(below, inverse)
    group = lax.broadcasted_iota(jnp.int32, product.shape, 0) // slab
    return jnp.where(group == panel, jnp.tile(own_rows, (below.shape[0] // slab, 1)), product)


def shared_slots(lower, whole, part, below, inverse, on_first, panel, panel_core, sources, cores):
    return spread(operator_of(lower, whole, part, panel), sources)


def own_slots(lower, whole, part, below, inverse, on_first, panel, panel_core, sources, cores):
    whole = sent_to_all(inverse, ROW).reshape(-1, inverse.shape[1])
    mine, other = halves(operator_of(below, whole, inverse, panel_core), on_first, 1)
    mine, other = spread(mine, sources), spread(swapped(other), sources)
    here = [(c == 0) == on_first for c in cores]
    return jnp.stack([jnp.where(h, mine[k], other[k]) for k, h in enumerate(here)])


def per_device(rhs_block, below, inverse, owner_map, row_perm):
    rows_dev, columns = rhs_block.shape
    below, inverse = below[0], inverse[0]
    slab, pivots = inverse.shape
    position = lax.axis_index(ROW)
    core = lax.axis_index("core")
    on_first = core == 0
    nz, nx = lax.axis_size("z"), lax.axis_size("x")
    chip = (lax.axis_index("x") * nz + lax.axis_index("z")).astype(jnp.uint32)

    owners = [owner_map[k].astype(jnp.uint32) for k in range(PANELS)]
    chips = [o >> 1 for o in owners]
    cores = [(o & 1).astype(jnp.int32) for o in owners]
    twice = (chips[0] == chips[1]) | (chips[0] == chips[2]) | (chips[1] == chips[2])
    held = [h == chip for h in chips]
    own_core = jnp.where(held[0], cores[0], jnp.where(held[1], cores[1], cores[2]))
    panel = jnp.where(held[0], 0, jnp.where(held[1], 1, 2))
    panel_core = jnp.where(
        held[0] & (cores[0] == core), 0, jnp.where(held[1] & (cores[1] == core), 1, 2)
    )
    sources = [(h % nz) * nx + h // nz for h in chips]

    kept, sent = halves(inverse, on_first, 1)
    part = jnp.where(own_core == core, kept, swapped(sent))
    lower = jnp.where(own_core == core, below, swapped(below))
    whole = sent_to_all(part, ROW).reshape(pivots, -1)
    kept = lax.cond(
        twice,
        own_slots,
        shared_slots,
        lower,
        whole,
        part,
        below,
        inverse,
        on_first,
        panel,
        panel_core,
        sources,
        cores,
    )

    def permuted(start, end):
        rows = row_perm[start:end] - position * rows_dev
        return rhs_block.at[rows].get(mode="promise_in_bounds")

    def to_all_rows(rows):
        return halves(sent_to_all(rows, ROW).reshape(pivots, columns), on_first, 0)

    def product(a, b):
        return dot(a[0], b[0]) + dot(a[1], b[1])

    kept = sent_to_all(kept, "z")
    pivot = [to_all_rows(permuted(0, slab))]
    working = permuted(slab, rows_dev)
    pairs = [(g, k) for g in range(PANELS) for k in range(g + 1)]
    first = jnp.stack([kept[g, k] for g, k in pairs])
    first = lax.all_gather(first, "x", axis=1, tiled=True)
    first = first, swapped(first)

    def own_group(g, k):
        return [f[pairs.index((g, k))] for f in first]

    rest = lax.all_gather(kept[PANELS:].swapaxes(0, 1), "x", axis=2, tiled=True)
    rest = rest.reshape(PANELS, -1, pivots // 2)
    rest = rest, swapped(rest)

    rows = [working[g * slab : (g + 1) * slab] for g in range(PANELS - 1)]
    tail = working[(PANELS - 1) * slab :]
    solved = []

    rows[0] = rows[0] + product(own_group(1, 0), pivot[0])
    rows, first, pivot = lax.optimization_barrier((rows, first, pivot))
    pivot.append(to_all_rows(rows[0]))
    solved.append(product(own_group(0, 0), pivot[0]))
    rows[1] = rows[1] + product(own_group(2, 0), pivot[0])
    tail = tail + product([r[0] for r in rest], pivot[0])
    rows[1] = rows[1] + product(own_group(2, 1), pivot[1])
    rows, tail, solved = lax.optimization_barrier((rows, tail, solved))
    pivot.append(to_all_rows(rows[1]))
    pivot, first, rest, tail = lax.optimization_barrier((pivot, first, rest, tail))
    for k in range(1, PANELS):
        solved.append(product(own_group(k, k), pivot[k]))
        tail = tail + product([r[k] for r in rest], pivot[k])
    return jnp.concatenate([*solved, tail])


def solution(mesh):
    mesh4 = Mesh(mesh.devices.reshape(4, 8, 2, 8), ("x", "z", "core", "row"))
    rhs = ("x", "z", "core")

    def step(*args):
        return per_device(*args)

    step = jax.shard_map(
        step,
        mesh=mesh4,
        in_specs=(P("row", rhs), P(rhs, "row", None), P(rhs, "row", None), P(), P("row")),
        out_specs=P("row", rhs),
        check_vma=False,
    )
    return step
```

```python
import jax
import jax.numpy as jnp
from jax import lax
from jax.sharding import Mesh, PartitionSpec as P


PANELS = 3
ROW = "row"
CHIP = ("z", "x")
SWAP = [(0, 1), (1, 0)]


def sent_to_all(x, axis):
    count = lax.axis_size(axis)
    return lax.all_to_all(jnp.broadcast_to(x[None], (count, *x.shape)), axis, 0, 0, tiled=True)


def swapped(x):
    return lax.ppermute(x, "core", SWAP)


def dot(a, b):
    return jnp.dot(a, b, precision=lax.Precision.HIGHEST, preferred_element_type=jnp.float32)


def halves(x, on_first, axis):
    low, high = jnp.split(x, 2, axis)
    return jnp.where(on_first, low, high), jnp.where(on_first, high, low)


def spread(operator, sources):
    rows, columns = operator.shape
    count = lax.axis_size(CHIP)
    operator, sources = lax.optimization_barrier((operator, sources))
    pieces = lax.all_to_all(
        operator.reshape(count, rows // count, columns), CHIP, 0, 0, tiled=True
    )
    return jnp.stack([lax.dynamic_index_in_dim(pieces, s, 0, keepdims=False) for s in sources])


def operator_of(below, inverse, own_rows, panel):
    slab = own_rows.shape[0]
    product = -dot(below, inverse)
    group = lax.broadcasted_iota(jnp.int32, product.shape, 0) // slab
    return jnp.where(group == panel, jnp.tile(own_rows, (below.shape[0] // slab, 1)), product)


def shared_slots(lower, whole, part, below, inverse, on_first, panel, panel_core, sources, cores):
    return spread(operator_of(lower, whole, part, panel), sources)


def own_slots(lower, whole, part, below, inverse, on_first, panel, panel_core, sources, cores):
    whole = sent_to_all(inverse, ROW).reshape(-1, inverse.shape[1])
    mine, other = halves(operator_of(below, whole, inverse, panel_core), on_first, 1)
    mine, other = spread(mine, sources), spread(swapped(other), sources)
    here = [(c == 0) == on_first for c in cores]
    return jnp.stack([jnp.where(h, mine[k], other[k]) for k, h in enumerate(here)])


def per_device(rhs_block, below, inverse, owner_map, row_perm):
    rows_dev, columns = rhs_block.shape
    below, inverse = below[0], inverse[0]
    slab, pivots = inverse.shape
    position = lax.axis_index(ROW)
    core = lax.axis_index("core")
    on_first = core == 0
    nz, nx = lax.axis_size("z"), lax.axis_size("x")
    chip = (lax.axis_index("x") * nz + lax.axis_index("z")).astype(jnp.uint32)

    owners = [owner_map[k].astype(jnp.uint32) for k in range(PANELS)]
    chips = [o >> 1 for o in owners]
    cores = [(o & 1).astype(jnp.int32) for o in owners]
    twice = (chips[0] == chips[1]) | (chips[0] == chips[2]) | (chips[1] == chips[2])
    held = [h == chip for h in chips]
    own_core = jnp.where(held[0], cores[0], jnp.where(held[1], cores[1], cores[2]))
    panel = jnp.where(held[0], 0, jnp.where(held[1], 1, 2))
    panel_core = jnp.where(
        held[0] & (cores[0] == core), 0, jnp.where(held[1] & (cores[1] == core), 1, 2)
    )
    sources = [(h % nz) * nx + h // nz for h in chips]

    kept, sent = halves(inverse, on_first, 1)
    part = jnp.where(own_core == core, kept, swapped(sent))
    lower = jnp.where(own_core == core, below, swapped(below))
    whole = sent_to_all(part, ROW).reshape(pivots, -1)
    lower, whole = lax.optimization_barrier((lower, whole))
    kept = lax.cond(
        twice,
        own_slots,
        shared_slots,
        lower,
        whole,
        part,
        below,
        inverse,
        on_first,
        panel,
        panel_core,
        sources,
        cores,
    )

    def permuted(start, end):
        rows = row_perm[start:end] - position * rows_dev
        return rhs_block.at[rows].get(mode="promise_in_bounds")

    def to_all_rows(rows):
        return halves(sent_to_all(rows, ROW).reshape(pivots, columns), on_first, 0)

    def product(a, b):
        return dot(a[0], b[0]) + dot(a[1], b[1])

    kept = sent_to_all(kept, "z")
    pivot = [to_all_rows(permuted(0, slab))]
    working = permuted(slab, rows_dev)
    pairs = [(g, k) for g in range(PANELS) for k in range(g + 1)]
    first = jnp.stack([kept[g, k] for g, k in pairs])
    first = lax.all_gather(first, "x", axis=1, tiled=True)
    first = first, swapped(first)

    def own_group(g, k):
        return [f[pairs.index((g, k))] for f in first]

    rows = [working[g * slab : (g + 1) * slab] for g in range(PANELS - 1)]
    tail = working[(PANELS - 1) * slab :]
    rows[0] = rows[0] + product(own_group(1, 0), pivot[0])
    rows, first, pivot, kept = lax.optimization_barrier((rows, first, pivot, kept))

    rest = lax.all_gather(kept[PANELS:].swapaxes(0, 1), "x", axis=2, tiled=True)
    rest = rest.reshape(PANELS, -1, pivots // 2)
    rest = rest, swapped(rest)
    pivot.append(to_all_rows(rows[0]))
    rows[1] = rows[1] + product(own_group(2, 0), pivot[0])
    rows[1] = rows[1] + product(own_group(2, 1), pivot[1])
    rows, first, pivot = lax.optimization_barrier((rows, first, pivot))
    pivot.append(to_all_rows(rows[1]))
    solved = []
    for k in range(PANELS):
        solved.append(product(own_group(k, k), pivot[k]))
        tail = tail + product([r[k] for r in rest], pivot[k])
    return jnp.concatenate([*solved, tail])


def solution(mesh):
    mesh4 = Mesh(mesh.devices.reshape(4, 8, 2, 8), ("x", "z", "core", "row"))
    rhs = ("x", "z", "core")

    def step(*args):
        return per_device(*args)

    step = jax.shard_map(
        step,
        mesh=mesh4,
        in_specs=(P("row", rhs), P(rhs, "row", None), P(rhs, "row", None), P(), P("row")),
        out_specs=P("row", rhs),
        check_vma=False,
    )
    return step
```

```python
import jax
import jax.numpy as jnp
from jax import lax
from jax.sharding import Mesh, PartitionSpec as P


PANELS = 3
ROW = "row"
CHIP = ("z", "x")
SWAP = [(0, 1), (1, 0)]


def sent_to_all(x, axis):
    count = lax.axis_size(axis)
    return lax.all_to_all(jnp.broadcast_to(x[None], (count, *x.shape)), axis, 0, 0, tiled=True)


def swapped(x):
    return lax.ppermute(x, "core", SWAP)


def dot(a, b):
    return jnp.dot(a, b, precision=lax.Precision.HIGHEST, preferred_element_type=jnp.float32)


def halves(x, on_first, axis):
    low, high = jnp.split(x, 2, axis)
    return jnp.where(on_first, low, high), jnp.where(on_first, high, low)


def spread(operators, sources):
    count = lax.axis_size(CHIP)
    sent = [o.reshape(count, 1, -1, o.shape[1]) for o in operators]
    sent, sources = lax.optimization_barrier((sent, sources))
    pieces = lax.all_to_all(jnp.concatenate(sent, axis=1), CHIP, 0, 0, tiled=True)
    return [lax.dynamic_index_in_dim(pieces, s, 0, keepdims=False) for s in sources]


def operator_of(below, inverse, own_rows, panel):
    slab = own_rows.shape[0]
    product = -dot(below, inverse)
    group = lax.broadcasted_iota(jnp.int32, product.shape, 0) // slab
    return jnp.where(group == panel, jnp.tile(own_rows, (below.shape[0] // slab, 1)), product)


def one_slot(main, whole, spare, mine, panels, sources, is_main):
    lower, part = main
    return jnp.stack([p[0] for p in spread([operator_of(lower, whole, part, panels[0])], sources)])


def two_slots(main, whole, spare, mine, panels, sources, is_main):
    lower, part = main
    operators = [operator_of(lower, whole, part, panels[0])]
    lower, part = (jnp.where(mine, got, kept) for kept, got in spare)
    whole = sent_to_all(part, ROW).reshape(whole.shape)
    operators.append(operator_of(lower, whole, part, panels[1]))
    pieces = spread(operators, sources)
    return jnp.stack([jnp.where(m, p[0], p[1]) for m, p in zip(is_main, pieces)])


def per_device(rhs_block, below, inverse, owner_map, row_perm):
    rows_dev, columns = rhs_block.shape
    below, inverse = below[0], inverse[0]
    slab, pivots = inverse.shape
    position = lax.axis_index(ROW)
    core = lax.axis_index("core")
    on_first = core == 0
    nz, nx = lax.axis_size("z"), lax.axis_size("x")
    chip = (lax.axis_index("x") * nz + lax.axis_index("z")).astype(jnp.uint32)

    owners = [owner_map[k].astype(jnp.uint32) for k in range(PANELS)]
    chips = [o >> 1 for o in owners]
    cores = [(o & 1).astype(jnp.int32) for o in owners]
    held = [h == chip for h in chips]
    own_core = jnp.where(held[0], cores[0], jnp.where(held[1], cores[1], cores[2]))
    panels = [
        jnp.where(held[0], 0, jnp.where(held[1], 1, 2)),
        jnp.where(held[2], 2, jnp.where(held[1], 1, 0)),
    ]
    is_main = [
        chips[0] == chips[0],
        chips[1] != chips[0],
        (chips[2] != chips[0]) & (chips[2] != chips[1]),
    ]
    sources = [(h % nz) * nx + h // nz for h in chips]

    mine = own_core == core
    kept, sent = halves(inverse, on_first, 1)
    got = swapped(sent)
    part = jnp.where(mine, kept, got)
    got_below = swapped(below)
    lower = jnp.where(mine, below, got_below)
    whole = sent_to_all(part, ROW).reshape(pivots, -1)
    lower, whole = lax.optimization_barrier((lower, whole))
    spare = (below, got_below), (kept, got)
    kept = lax.cond(
        ~(is_main[1] & is_main[2]),
        two_slots,
        one_slot,
        (lower, part),
        whole,
        spare,
        mine,
        panels,
        sources,
        is_main,
    )

    def permuted(start, end):
        rows = row_perm[start:end] - position * rows_dev
        return rhs_block.at[rows].get(mode="promise_in_bounds")

    def to_all_rows(rows):
        return halves(sent_to_all(rows, ROW).reshape(pivots, columns), on_first, 0)

    def product(a, b):
        return dot(a[0], b[0]) + dot(a[1], b[1])

    kept = sent_to_all(kept, "z")
    pivot = [to_all_rows(permuted(0, slab))]
    working = permuted(slab, rows_dev)
    pairs = [(g, k) for g in range(PANELS) for k in range(g + 1)]
    first = jnp.stack([kept[g, k] for g, k in pairs])
    first = lax.all_gather(first, "x", axis=1, tiled=True)
    first = first, swapped(first)

    def own_group(g, k):
        return [f[pairs.index((g, k))] for f in first]

    rest = lax.all_gather(kept[PANELS:].swapaxes(0, 1), "x", axis=2, tiled=True)
    rest = rest.reshape(PANELS, -1, pivots // 2)
    rest = rest, swapped(rest)

    rows = [working[g * slab : (g + 1) * slab] for g in range(PANELS - 1)]
    tail = working[(PANELS - 1) * slab :]
    solved = []

    rows[0] = rows[0] + product(own_group(1, 0), pivot[0])
    rows, first, pivot = lax.optimization_barrier((rows, first, pivot))
    pivot.append(to_all_rows(rows[0]))
    solved.append(product(own_group(0, 0), pivot[0]))
    rows[1] = rows[1] + product(own_group(2, 0), pivot[0])
    tail = tail + product([r[0] for r in rest], pivot[0])
    rows[1] = rows[1] + product(own_group(2, 1), pivot[1])
    rows, tail, solved = lax.optimization_barrier((rows, tail, solved))
    pivot.append(to_all_rows(rows[1]))
    pivot, first, rest, tail = lax.optimization_barrier((pivot, first, rest, tail))
    for k in range(1, PANELS):
        solved.append(product(own_group(k, k), pivot[k]))
        tail = tail + product([r[k] for r in rest], pivot[k])
    return jnp.concatenate([*solved, tail])


def solution(mesh):
    mesh4 = Mesh(mesh.devices.reshape(4, 8, 2, 8), ("x", "z", "core", "row"))
    rhs = ("x", "z", "core")

    def step(*args):
        return per_device(*args)

    step = jax.shard_map(
        step,
        mesh=mesh4,
        in_specs=(P("row", rhs), P(rhs, "row", None), P(rhs, "row", None), P(), P("row")),
        out_specs=P("row", rhs),
        check_vma=False,
    )
    return step
```

```python
import jax
import jax.numpy as jnp
from jax import lax
from jax.sharding import Mesh, PartitionSpec as P


PANELS = 3
ROW = "row"
CHIP = ("z", "x")
SWAP = [(0, 1), (1, 0)]


def sent_to_all(x, axis):
    count = lax.axis_size(axis)
    return lax.all_to_all(jnp.broadcast_to(x[None], (count, *x.shape)), axis, 0, 0, tiled=True)


def swapped(x):
    return lax.ppermute(x, "core", SWAP)


def dot(a, b):
    return jnp.dot(a, b, precision=lax.Precision.HIGHEST, preferred_element_type=jnp.float32)


def halves(x, on_first, axis):
    low, high = jnp.split(x, 2, axis)
    return jnp.where(on_first, low, high), jnp.where(on_first, high, low)


def spread(operators, sources):
    count = lax.axis_size(CHIP)
    sent = [o.reshape(count, 1, -1, o.shape[1]) for o in operators]
    sent, sources = lax.optimization_barrier((sent, sources))
    pieces = lax.all_to_all(jnp.concatenate(sent, axis=1), CHIP, 0, 0, tiled=True)
    return [lax.dynamic_index_in_dim(pieces, s, 0, keepdims=False) for s in sources]


def operator_of(below, inverse, own_rows, panel):
    slab = own_rows.shape[0]
    product = -dot(below, inverse)
    group = lax.broadcasted_iota(jnp.int32, product.shape, 0) // slab
    return jnp.where(group == panel, jnp.tile(own_rows, (below.shape[0] // slab, 1)), product)


def one_slot(main, whole, spare, mine, panels, sources, is_main):
    lower, part = main
    return jnp.stack([p[0] for p in spread([operator_of(lower, whole, part, panels[0])], sources)])


def two_slots(main, whole, spare, mine, panels, sources, is_main):
    lower, part = main
    operators = [operator_of(lower, whole, part, panels[0])]
    lower, part = (jnp.where(mine, got, kept) for kept, got in spare)
    whole = sent_to_all(part, ROW).reshape(whole.shape)
    operators.append(operator_of(lower, whole, part, panels[1]))
    pieces = spread(operators, sources)
    return jnp.stack([jnp.where(m, p[0], p[1]) for m, p in zip(is_main, pieces)])


def per_device(rhs_block, below, inverse, owner_map, row_perm):
    rows_dev, columns = rhs_block.shape
    below, inverse = below[0], inverse[0]
    slab, pivots = inverse.shape
    position = lax.axis_index(ROW)
    core = lax.axis_index("core")
    on_first = core == 0
    nz, nx = lax.axis_size("z"), lax.axis_size("x")
    chip = (lax.axis_index("x") * nz + lax.axis_index("z")).astype(jnp.uint32)

    owners = [owner_map[k] for k in range(PANELS)]
    me = (lax.axis_index("x") * nz + lax.axis_index("z")) * 2 + core
    first_mine, second_mine, third_mine = (o == me for o in owners)
    mine = first_mine | (
        (owners[0] != me ^ 1) & (second_mine | ((owners[1] != me ^ 1) & third_mine))
    )
    owners = [o.astype(jnp.uint32) for o in owners]
    chips = [o >> 1 for o in owners]
    held = [h == chip for h in chips]
    panels = [
        jnp.where(held[0], 0, jnp.where(held[1], 1, 2)),
        jnp.where(held[2], 2, jnp.where(held[1], 1, 0)),
    ]
    is_main = [
        chips[0] == chips[0],
        chips[1] != chips[0],
        (chips[2] != chips[0]) & (chips[2] != chips[1]),
    ]
    sources = [(h % nz) * nx + h // nz for h in chips]

    kept, sent = halves(inverse, on_first, 1)
    got = swapped(sent)
    part = jnp.where(mine, kept, got)
    got_below = swapped(below)
    lower = jnp.where(mine, below, got_below)
    whole = sent_to_all(part, ROW).reshape(pivots, -1)
    lower, whole = lax.optimization_barrier((lower, whole))
    spare = (below, got_below), (kept, got)
    kept = lax.cond(
        ~(is_main[1] & is_main[2]),
        two_slots,
        one_slot,
        (lower, part),
        whole,
        spare,
        mine,
        panels,
        sources,
        is_main,
    )

    def permuted(start, end):
        rows = row_perm[start:end] - position * rows_dev
        return rhs_block.at[rows].get(mode="promise_in_bounds")

    def to_all_rows(rows):
        return halves(sent_to_all(rows, ROW).reshape(pivots, columns), on_first, 0)

    def product(a, b):
        return dot(a[0], b[0]) + dot(a[1], b[1])

    kept = sent_to_all(kept, "z")
    pivot = [to_all_rows(permuted(0, slab))]
    working = permuted(slab, rows_dev)
    pairs = [(g, k) for g in range(PANELS) for k in range(g + 1)]
    first = jnp.stack([kept[g, k] for g, k in pairs])
    first = lax.all_gather(first, "x", axis=1, tiled=True)
    first = first, swapped(first)

    def own_group(g, k):
        return [f[pairs.index((g, k))] for f in first]

    rest = lax.all_gather(kept[PANELS:].swapaxes(0, 1), "x", axis=2, tiled=True)
    rest = rest.reshape(PANELS, -1, pivots // 2)
    rest = rest, swapped(rest)

    rows = [working[g * slab : (g + 1) * slab] for g in range(PANELS - 1)]
    tail = working[(PANELS - 1) * slab :]
    solved = []

    rows[0] = rows[0] + product(own_group(1, 0), pivot[0])
    rows, first, pivot = lax.optimization_barrier((rows, first, pivot))
    pivot.append(to_all_rows(rows[0]))
    rows[1] = rows[1] + product(own_group(2, 0), pivot[0])
    rows[1] = rows[1] + product(own_group(2, 1), pivot[1])
    rows, first, pivot, rest, tail = lax.optimization_barrier((rows, first, pivot, rest, tail))
    pivot.append(to_all_rows(rows[1]))
    for k in range(PANELS - 1):
        solved.append(product(own_group(k, k), pivot[k]))
        tail = tail + product([r[k] for r in rest], pivot[k])
    pivot, first, rest, tail = lax.optimization_barrier((pivot, first, rest, tail))
    solved.append(product(own_group(PANELS - 1, PANELS - 1), pivot[-1]))
    tail = tail + product([r[-1] for r in rest], pivot[-1])
    return jnp.concatenate([*solved, tail])


def solution(mesh):
    mesh4 = Mesh(mesh.devices.reshape(4, 8, 2, 8), ("x", "z", "core", "row"))
    rhs = ("x", "z", "core")

    def step(*args):
        return per_device(*args)

    step = jax.shard_map(
        step,
        mesh=mesh4,
        in_specs=(P("row", rhs), P(rhs, "row", None), P(rhs, "row", None), P(), P("row")),
        out_specs=P("row", rhs),
        check_vma=False,
    )
    return step
```

```python
import jax
import jax.numpy as jnp
from jax import lax
from jax.sharding import Mesh, PartitionSpec as P


PANELS = 3
ROW = "row"
CHIP = ("z", "x")
SWAP = [(0, 1), (1, 0)]


def sent_to_all(x, axis):
    count = lax.axis_size(axis)
    return lax.all_to_all(jnp.broadcast_to(x[None], (count, *x.shape)), axis, 0, 0, tiled=True)


def swapped(x):
    return lax.ppermute(x, "core", SWAP)


def dot(a, b):
    return jnp.dot(a, b, precision=lax.Precision.HIGHEST, preferred_element_type=jnp.float32)


def halves(x, on_first, axis):
    low, high = jnp.split(x, 2, axis)
    return jnp.where(on_first, low, high), jnp.where(on_first, high, low)


def spread(operators, sources):
    count = lax.axis_size(CHIP)
    sent = [o.reshape(count, 1, -1, o.shape[1]) for o in operators]
    sent, sources = lax.optimization_barrier((sent, sources))
    pieces = lax.all_to_all(jnp.concatenate(sent, axis=1), CHIP, 0, 0, tiled=True)
    return [lax.dynamic_index_in_dim(pieces, s, 0, keepdims=False) for s in sources]


def operator_of(below, inverse, own_rows, panel):
    slab = own_rows.shape[0]
    product = -dot(below, inverse)
    group = lax.broadcasted_iota(jnp.int32, product.shape, 0) // slab
    return jnp.where(group == panel, jnp.tile(own_rows, (below.shape[0] // slab, 1)), product)


def one_slot(main, whole, spare, mine, panels, sources, is_main):
    lower, part = main
    return jnp.stack([p[0] for p in spread([operator_of(lower, whole, part, panels[0])], sources)])


def two_slots(main, whole, spare, mine, panels, sources, is_main):
    lower, part = main
    operators = [operator_of(lower, whole, part, panels[0])]
    lower, part = (jnp.where(mine, got, kept) for kept, got in spare)
    whole = sent_to_all(part, ROW).reshape(whole.shape)
    operators.append(operator_of(lower, whole, part, panels[1]))
    pieces = spread(operators, sources)
    return jnp.stack([jnp.where(m, p[0], p[1]) for m, p in zip(is_main, pieces)])


def per_device(rhs_block, below, inverse, owner_map, row_perm):
    rows_dev, columns = rhs_block.shape
    below, inverse = below[0], inverse[0]
    slab, pivots = inverse.shape
    position = lax.axis_index(ROW)
    core = lax.axis_index("core")
    on_first = core == 0
    nz, nx = lax.axis_size("z"), lax.axis_size("x")
    chip = (lax.axis_index("x") * nz + lax.axis_index("z")).astype(jnp.uint32)

    owners = [owner_map[k].astype(jnp.uint32) for k in range(PANELS)]
    chips = [o >> 1 for o in owners]
    cores = [(o & 1).astype(jnp.int32) for o in owners]
    held = [h == chip for h in chips]
    own_core = jnp.where(held[0], cores[0], jnp.where(held[1], cores[1], cores[2]))
    mine = own_core == core
    panels = [
        jnp.where(held[0], 0, jnp.where(held[1], 1, 2)),
        jnp.where(held[2], 2, jnp.where(held[1], 1, 0)),
    ]
    is_main = [
        chips[0] == chips[0],
        chips[1] != chips[0],
        (chips[2] != chips[0]) & (chips[2] != chips[1]),
    ]
    sources = [(h % nz) * nx + h // nz for h in chips]

    kept, sent = halves(inverse, on_first, 1)
    got = swapped(sent)
    part = jnp.where(mine, kept, got)
    got_below = swapped(below)
    lower = jnp.where(mine, below, got_below)
    whole = sent_to_all(part, ROW).reshape(pivots, -1)
    lower, whole = lax.optimization_barrier((lower, whole))
    spare = (below, got_below), (kept, got)
    kept = lax.cond(
        ~(is_main[1] & is_main[2]),
        two_slots,
        one_slot,
        (lower, part),
        whole,
        spare,
        mine,
        panels,
        sources,
        is_main,
    )

    def permuted(start, end):
        rows = row_perm[start:end] - position * rows_dev
        return rhs_block.at[rows].get(mode="promise_in_bounds")

    def to_all_rows(rows):
        return halves(sent_to_all(rows, ROW).reshape(pivots, columns), on_first, 0)

    def product(a, b):
        return dot(a[0], b[0]) + dot(a[1], b[1])

    kept = sent_to_all(kept, "z")
    pivot = [to_all_rows(permuted(0, slab))]
    working = permuted(slab, rows_dev)
    pairs = [(g, k) for g in range(PANELS) for k in range(g + 1)]
    first = jnp.stack([kept[g, k] for g, k in pairs])
    first = lax.all_gather(first, "x", axis=1, tiled=True)
    first = first, swapped(first)

    def own_group(g, k):
        return [f[pairs.index((g, k))] for f in first]

    rest = lax.all_gather(kept[PANELS:].swapaxes(0, 1), "x", axis=2, tiled=True)
    rest = rest.reshape(PANELS, -1, pivots // 2)
    rest = rest, swapped(rest)

    rows = [working[g * slab : (g + 1) * slab] for g in range(PANELS - 1)]
    tail = working[(PANELS - 1) * slab :]
    solved = []

    rows[0] = rows[0] + product(own_group(1, 0), pivot[0])
    rows, first, pivot = lax.optimization_barrier((rows, first, pivot))
    pivot.append(to_all_rows(rows[0]))
    rows[1] = rows[1] + product(own_group(2, 0), pivot[0])
    rows, pivot, last = lax.optimization_barrier((rows, pivot, own_group(2, 1)))
    rows[1] = rows[1] + product(last, pivot[1])
    rows, first, pivot, rest, tail = lax.optimization_barrier((rows, first, pivot, rest, tail))
    pivot.append(to_all_rows(rows[1]))
    for k in range(PANELS - 1):
        solved.append(product(own_group(k, k), pivot[k]))
        tail = tail + product([r[k] for r in rest], pivot[k])
    last = own_group(PANELS - 1, PANELS - 1), [r[-1] for r in rest]
    pivot, last, tail = lax.optimization_barrier((pivot, last, tail))
    solved.append(product(last[0], pivot[-1]))
    tail = tail + product(last[1], pivot[-1])
    return jnp.concatenate([*solved, tail])


def solution(mesh):
    mesh4 = Mesh(mesh.devices.reshape(4, 8, 2, 8), ("x", "z", "core", "row"))
    rhs = ("x", "z", "core")

    def step(*args):
        return per_device(*args)

    step = jax.shard_map(
        step,
        mesh=mesh4,
        in_specs=(P("row", rhs), P(rhs, "row", None), P(rhs, "row", None), P(), P("row")),
        out_specs=P("row", rhs),
        check_vma=False,
    )
    return step
```

```python
import jax
import jax.numpy as jnp
from jax import lax
from jax.sharding import Mesh, PartitionSpec as P


PANELS = 3
ROW = "row"
CHIP = ("z", "x")
SWAP = [(0, 1), (1, 0)]


def sent_to_all(x, axis):
    count = lax.axis_size(axis)
    return lax.all_to_all(jnp.broadcast_to(x[None], (count, *x.shape)), axis, 0, 0, tiled=True)


def sent_to_all_rows_reversed(x):
    count = lax.axis_size(ROW)
    tiles = jnp.broadcast_to(x[None], (count, *x.shape))
    groups = [list(range(count))[::-1]]
    return lax.all_to_all(tiles, ROW, 0, 0, tiled=True, axis_index_groups=groups)[::-1]


def swapped(x):
    return lax.ppermute(x, "core", SWAP)


def dot(a, b):
    return jnp.dot(a, b, precision=lax.Precision.HIGHEST, preferred_element_type=jnp.float32)


def halves(x, on_first, axis):
    low, high = jnp.split(x, 2, axis)
    return jnp.where(on_first, low, high), jnp.where(on_first, high, low)


def spread(operators, sources):
    count = lax.axis_size(CHIP)
    sent = [o.reshape(count, 1, -1, o.shape[1]) for o in operators]
    sent, sources = lax.optimization_barrier((sent, sources))
    pieces = lax.all_to_all(jnp.concatenate(sent, axis=1), CHIP, 0, 0, tiled=True)
    return [lax.dynamic_index_in_dim(pieces, s, 0, keepdims=False) for s in sources]


def operator_of(below, inverse, own_rows, panel):
    slab = own_rows.shape[0]
    product = -dot(below, inverse)
    group = lax.broadcasted_iota(jnp.int32, product.shape, 0) // slab
    return jnp.where(group == panel, jnp.tile(own_rows, (below.shape[0] // slab, 1)), product)


def one_slot(main, whole, spare, mine, panels, sources, is_main):
    lower, part = main
    return jnp.stack([p[0] for p in spread([operator_of(lower, whole, part, panels[0])], sources)])


def two_slots(main, whole, spare, mine, panels, sources, is_main):
    lower, part = main
    operators = [operator_of(lower, whole, part, panels[0])]
    lower, part = (jnp.where(mine, got, kept) for kept, got in spare)
    whole = sent_to_all(part, ROW).reshape(whole.shape)
    operators.append(operator_of(lower, whole, part, panels[1]))
    pieces = spread(operators, sources)
    return jnp.stack([jnp.where(m, p[0], p[1]) for m, p in zip(is_main, pieces)])


def per_device(rhs_block, below, inverse, owner_map, row_perm):
    rows_dev, columns = rhs_block.shape
    below, inverse = below[0], inverse[0]
    slab, pivots = inverse.shape
    position = lax.axis_index(ROW)
    core = lax.axis_index("core")
    on_first = core == 0
    nz, nx = lax.axis_size("z"), lax.axis_size("x")
    chip = (lax.axis_index("x") * nz + lax.axis_index("z")).astype(jnp.uint32)

    owners = [owner_map[k].astype(jnp.uint32) for k in range(PANELS)]
    chips = [o >> 1 for o in owners]
    cores = [(o & 1).astype(jnp.int32) for o in owners]
    held = [h == chip for h in chips]
    own_core = jnp.where(held[0], cores[0], jnp.where(held[1], cores[1], cores[2]))
    mine = own_core == core
    panels = [
        jnp.where(held[0], 0, jnp.where(held[1], 1, 2)),
        jnp.where(held[2], 2, jnp.where(held[1], 1, 0)),
    ]
    is_main = [
        chips[0] == chips[0],
        chips[1] != chips[0],
        (chips[2] != chips[0]) & (chips[2] != chips[1]),
    ]
    sources = [(h % nz) * nx + h // nz for h in chips]

    kept, sent = halves(inverse, on_first, 1)
    got = swapped(sent)
    part = jnp.where(mine, kept, got)
    got_below = swapped(below)
    lower = jnp.where(mine, below, got_below)
    whole = sent_to_all(part, ROW).reshape(pivots, -1)
    lower, whole = lax.optimization_barrier((lower, whole))
    spare = (below, got_below), (kept, got)
    kept = lax.cond(
        ~(is_main[1] & is_main[2]),
        two_slots,
        one_slot,
        (lower, part),
        whole,
        spare,
        mine,
        panels,
        sources,
        is_main,
    )

    def permuted(start, end):
        rows = row_perm[start:end] - position * rows_dev
        return rhs_block.at[rows].get(mode="promise_in_bounds")

    def to_all_rows(rows, send=lambda x: sent_to_all(x, ROW)):
        return halves(send(rows).reshape(pivots, columns), on_first, 0)

    def product(a, b):
        return dot(a[0], b[0]) + dot(a[1], b[1])

    kept = sent_to_all(kept, "z")
    pivot = [to_all_rows(permuted(0, slab))]
    working = permuted(slab, rows_dev)
    pairs = [(g, k) for g in range(PANELS) for k in range(g + 1)]
    first = jnp.stack([kept[g, k] for g, k in pairs])
    first = lax.all_gather(first, "x", axis=1, tiled=True)
    first = first, swapped(first)

    def own_group(g, k):
        return [f[pairs.index((g, k))] for f in first]

    rest = lax.all_gather(kept[PANELS:].swapaxes(0, 1), "x", axis=2, tiled=True)
    rest = rest.reshape(PANELS, -1, pivots // 2)
    rest = rest, swapped(rest)

    rows = [working[g * slab : (g + 1) * slab] for g in range(PANELS - 1)]
    tail = working[(PANELS - 1) * slab :]
    solved = []

    rows[0] = rows[0] + product(own_group(1, 0), pivot[0])
    rows, first, pivot = lax.optimization_barrier((rows, first, pivot))
    pivot.append(to_all_rows(rows[0], sent_to_all_rows_reversed))
    rows[1] = rows[1] + product(own_group(2, 0), pivot[0])
    rows, pivot, last = lax.optimization_barrier((rows, pivot, own_group(2, 1)))
    rows[1] = rows[1] + product(last, pivot[1])
    rows, first, pivot, rest, tail = lax.optimization_barrier((rows, first, pivot, rest, tail))
    pivot.append(to_all_rows(rows[1]))
    for k in range(PANELS - 1):
        solved.append(product(own_group(k, k), pivot[k]))
        tail = tail + product([r[k] for r in rest], pivot[k])
    last = own_group(PANELS - 1, PANELS - 1), [r[-1] for r in rest]
    pivot, last, tail = lax.optimization_barrier((pivot, last, tail))
    solved.append(product(last[0], pivot[-1]))
    tail = tail + product(last[1], pivot[-1])
    return jnp.concatenate([*solved, tail])


def solution(mesh):
    mesh4 = Mesh(mesh.devices.reshape(4, 8, 2, 8), ("x", "z", "core", "row"))
    rhs = ("x", "z", "core")

    def step(*args):
        return per_device(*args)

    step = jax.shard_map(
        step,
        mesh=mesh4,
        in_specs=(P("row", rhs), P(rhs, "row", None), P(rhs, "row", None), P(), P("row")),
        out_specs=P("row", rhs),
        check_vma=False,
    )
    return step
```

```python
import jax
import jax.numpy as jnp
from jax import lax
from jax.sharding import Mesh, PartitionSpec as P


PANELS = 3
ROW = "row"
CHIP = ("z", "x")
SWAP = [(0, 1), (1, 0)]


def sent_to_all(x, axis):
    count = lax.axis_size(axis)
    return lax.all_to_all(jnp.broadcast_to(x[None], (count, *x.shape)), axis, 0, 0, tiled=True)


def swapped(x):
    return lax.ppermute(x, "core", SWAP)


def dot(a, b):
    return jnp.dot(a, b, precision=lax.Precision.HIGHEST, preferred_element_type=jnp.float32)


def halves(x, on_first, axis):
    low, high = jnp.split(x, 2, axis)
    return jnp.where(on_first, low, high), jnp.where(on_first, high, low)


def spread(operators, sources):
    count = lax.axis_size(CHIP)
    sent = [o.reshape(count, 1, -1, o.shape[1]) for o in operators]
    sent, sources = lax.optimization_barrier((sent, sources))
    pieces = lax.all_to_all(jnp.concatenate(sent, axis=1), CHIP, 0, 0, tiled=True)
    return [lax.dynamic_index_in_dim(pieces, s, 0, keepdims=False) for s in sources]


def operator_of(below, inverse, own_rows, panel):
    slab = own_rows.shape[0]
    product = -dot(below, inverse)
    group = lax.broadcasted_iota(jnp.int32, product.shape, 0) // slab
    return jnp.where(group == panel, jnp.tile(own_rows, (below.shape[0] // slab, 1)), product)


def one_slot(main, whole, spare, mine, panels, sources, is_main, pivot_rows):
    lower, part = main
    operator = operator_of(lower, whole, part, panels[0])
    pieces = spread([operator], sources)
    pivot = lax.all_gather(pivot_rows, ROW, tiled=True)
    return jnp.stack([p[0] for p in pieces]), pivot


def two_slots(main, whole, spare, mine, panels, sources, is_main, pivot_rows):
    lower, part = main
    operators = [operator_of(lower, whole, part, panels[0])]
    lower, part = (jnp.where(mine, got, kept) for kept, got in spare)
    whole = sent_to_all(part, ROW).reshape(whole.shape)
    operators.append(operator_of(lower, whole, part, panels[1]))
    pieces = spread(operators, sources)
    pivot = lax.all_gather(pivot_rows, ROW, tiled=True)
    return jnp.stack([jnp.where(m, p[0], p[1]) for m, p in zip(is_main, pieces)]), pivot


def per_device(rhs_block, below, inverse, owner_map, row_perm):
    rows_dev, columns = rhs_block.shape
    below, inverse = below[0], inverse[0]
    slab, pivots = inverse.shape
    position = lax.axis_index(ROW)
    core = lax.axis_index("core")
    on_first = core == 0
    nz, nx = lax.axis_size("z"), lax.axis_size("x")
    chip = (lax.axis_index("x") * nz + lax.axis_index("z")).astype(jnp.uint32)

    owners = [owner_map[k].astype(jnp.uint32) for k in range(PANELS)]
    chips = [o >> 1 for o in owners]
    cores = [(o & 1).astype(jnp.int32) for o in owners]
    held = [h == chip for h in chips]
    own_core = jnp.where(held[0], cores[0], jnp.where(held[1], cores[1], cores[2]))
    mine = own_core == core
    panels = [
        jnp.where(held[0], 0, jnp.where(held[1], 1, 2)),
        jnp.where(held[2], 2, jnp.where(held[1], 1, 0)),
    ]
    is_main = [
        chips[0] == chips[0],
        chips[1] != chips[0],
        (chips[2] != chips[0]) & (chips[2] != chips[1]),
    ]
    sources = [(h % nz) * nx + h // nz for h in chips]

    kept, sent = halves(inverse, on_first, 1)
    got = swapped(sent)
    part = jnp.where(mine, kept, got)
    got_below = swapped(below)
    lower = jnp.where(mine, below, got_below)
    whole = sent_to_all(part, ROW).reshape(pivots, -1)
    lower, whole = lax.optimization_barrier((lower, whole))
    spare = (below, got_below), (kept, got)

    def permuted(start, end):
        rows = row_perm[start:end] - position * rows_dev
        return rhs_block.at[rows].get(mode="promise_in_bounds")

    kept, pivot = lax.cond(
        ~(is_main[1] & is_main[2]),
        two_slots,
        one_slot,
        (lower, part),
        whole,
        spare,
        mine,
        panels,
        sources,
        is_main,
        permuted(0, slab),
    )

    def to_all_rows(rows):
        return halves(sent_to_all(rows, ROW).reshape(pivots, columns), on_first, 0)

    def product(a, b):
        return dot(a[0], b[0]) + dot(a[1], b[1])

    kept = sent_to_all(kept, "z")
    pivot = [halves(pivot, on_first, 0)]
    working = permuted(slab, rows_dev)
    pairs = [(g, k) for g in range(PANELS) for k in range(g + 1)]
    first = jnp.stack([kept[g, k] for g, k in pairs])
    first = lax.all_gather(first, "x", axis=1, tiled=True)
    first = first, swapped(first)

    def own_group(g, k):
        return [f[pairs.index((g, k))] for f in first]

    rest = lax.all_gather(kept[PANELS:].swapaxes(0, 1), "x", axis=2, tiled=True)
    rest = rest.reshape(PANELS, -1, pivots // 2)
    rest = rest, swapped(rest)

    rows = [working[g * slab : (g + 1) * slab] for g in range(PANELS - 1)]
    tail = working[(PANELS - 1) * slab :]
    solved = []

    rows[0] = rows[0] + product(own_group(1, 0), pivot[0])
    rows, first, pivot = lax.optimization_barrier((rows, first, pivot))
    pivot.append(to_all_rows(rows[0]))
    rows[1] = rows[1] + product(own_group(2, 0), pivot[0])
    rows, pivot, last = lax.optimization_barrier((rows, pivot, own_group(2, 1)))
    rows[1] = rows[1] + product(last, pivot[1])
    rows, first, pivot, rest, tail = lax.optimization_barrier((rows, first, pivot, rest, tail))
    pivot.append(to_all_rows(rows[1]))
    for k in range(PANELS - 1):
        solved.append(product(own_group(k, k), pivot[k]))
        tail = tail + product([r[k] for r in rest], pivot[k])
    last = own_group(PANELS - 1, PANELS - 1), [r[-1] for r in rest]
    pivot, last, tail = lax.optimization_barrier((pivot, last, tail))
    solved.append(product(last[0], pivot[-1]))
    tail = tail + product(last[1], pivot[-1])
    return jnp.concatenate([*solved, tail])


def solution(mesh):
    mesh4 = Mesh(mesh.devices.reshape(4, 8, 2, 8), ("x", "z", "core", "row"))
    rhs = ("x", "z", "core")

    def step(*args):
        return per_device(*args)

    step = jax.shard_map(
        step,
        mesh=mesh4,
        in_specs=(P("row", rhs), P(rhs, "row", None), P(rhs, "row", None), P(), P("row")),
        out_specs=P("row", rhs),
        check_vma=False,
    )
    return step
```
